256 devices in a mesh: expert: 8 (over y, core), tensor: 32 (over z, x).
Axes of the slice: x: 4, y: 4, z: 8, core: 2. Of those that a mesh axis runs over, the one named last changes fastest.
Arguments:
- tokens: bfloat16 [2048, 6144], P('expert', 'tensor'), may hold values from -6 to 6
- expert_ids: int32 [2048, 2], P('expert'), may hold values from 0 to 7, all different within a row; in each aligned block of 256 rows (0 to 255, 256 to 511, ...) at most 96 rows name the same one
- gate_prob: float32 [2048, 2], P('expert'), may hold values from 0.1 to 1
- w_gate: bfloat16 [8, 6144, 8192], P('expert', None, 'tensor'), may hold values from -0.078125 to 0.078125
- w_up: bfloat16 [8, 6144, 8192], P('expert', None, 'tensor'), may hold values from -0.078125 to 0.078125
- w_down: bfloat16 [8, 8192, 6144], P('expert', 'tensor'), may hold values from -0.125 to 0.125
Outputs:
- mixed: bfloat16 [2048, 6144], P('expert', 'tensor')
The draws below stay inside these ranges and needn't reach their ends.
Inputs may be any that keep to these rules, and one draw needn't show every extreme that they name: `expert_ids`: the two experts of a row differ. Within the rows of one index of expert (aligned blocks of 256 rows) no expert is named by more than 96 rows, and in every draw some expert is named by exactly 96 rows of some block.
All inputs are finite; a program needn't handle non-finite values.
Results may differ from the reference program's by a relative error of at most 0.017.
Values may be sent and summed in bfloat16 or wider, within the bound.
No kernel may reach another device: no remote copies, remote signals or barrier semaphores. Data moves between devices by JAX's collectives and lax.ppermute only.
A program may use at most 64 MiB of HBM per device.

```python
import math
import jax
import jax.numpy as jnp
import numpy as np
from jax import lax

D = 6144
FF = 8192
TOK_G = 256
EXPERTS = 8
CAP = 96
TOKENS = 2048
N_EXPERT = 8
N_TENSOR = 32


def with_spikes(entries, rng, source, target, shards_of, factor):
    owner, partner = [(jnp.arange(entries.shape[dim]) // (entries.shape[dim] // shards_of)).reshape([-1 if axis == dim else 1 for axis in range(entries.ndim)]) for dim in (source, target)]
    chosen = jax.random.permutation(rng, shards_of)[partner]
    strong = (owner == chosen) | (owner == (partner + shards_of // 2) % shards_of)
    return jnp.where(strong, factor * entries, entries)


def block_scale(key, dims, shards, low, largest):
    loudness = 1.0
    for dim, shards_of in shards:
        heights = jax.random.uniform(jax.random.fold_in(jax.random.fold_in(key, 6), dim), (shards_of,), jnp.float32, low / len(shards), largest / len(shards))
        loudness = loudness * jnp.repeat(jnp.exp(heights), dims[dim] // shards_of).reshape((-1,) + (1,) * (len(dims) - 1 - dim))
    return loudness


def shared_out(stream_key, own, number, rows, number_of, top, bound, skew):
    ranking = jax.random.permutation(stream_key, number_of)
    heavy_load, ordinary = shares(number_of, rows * top, bound, skew, True), shares(number_of, rows * top, bound, skew, False)
    places = jnp.arange(number_of)

    def named(sizes, rotation):
        used = int((sizes > 0).sum())
        fixed = max(1, used // 4)
        moved = fixed + (places - fixed + rotation * (used - fixed)) % max(1, number_of - fixed)
        return jnp.zeros((number_of,), jnp.int32).at[ranking[jnp.where(places < fixed, places, moved)]].set(jnp.asarray(sizes, jnp.int32))

    sizes = jnp.where(number % 4 == 0, named(heavy_load, number // 4), named(ordinary, number - number // 4 - 1))
    mixed = jax.random.permutation(jax.random.fold_in(own, 3), number_of)
    donor, sink = mixed[0:number_of // 2 * 2:2], mixed[1:number_of // 2 * 2:2]
    room = jnp.minimum(sizes[donor] - 1, bound - sizes[sink]) // 2
    room = jnp.where((donor == ranking[0]) | (sink == ranking[0]) | (sizes[sink] == 0), 0, jnp.maximum(room, 0))
    moved = jax.random.randint(jax.random.fold_in(own, 4), (number_of // 2,), 0, 1 << 20) % (room + 1)
    sizes = sizes.at[donor].add(-moved).at[sink].add(moved)
    members = jnp.searchsorted(jnp.cumsum(sizes), jnp.arange(rows * top), side="right").astype(jnp.int32)
    table = members.reshape(top, rows).T
    table = table[jax.random.permutation(jax.random.fold_in(own, 1), rows)]
    rotation = jax.random.randint(jax.random.fold_in(own, 2), (rows, 1), 0, top)
    return jnp.take_along_axis(table, (jnp.arange(top)[None, :] + rotation) % top, axis=1)


def shares(count, total, most, skew, full):
    weights = [(1 << 20) // math.isqrt(rank ** skew) + 1 for rank in range(1, count + 1)]
    largest = most if full else min(most, max(-(-total // count), total * weights[0] // sum(weights)))
    least = 1 if total - largest >= count - 1 else 0
    given, spare = [largest] + [least] * (count - 1), total - largest - least * (count - 1)
    while spare > 0:
        candidates = [i for i in range(1, count) if given[i] < largest] or [i for i in range(1, count) if given[i] < most]
        mass, budget = sum([weights[i] for i in candidates]), spare
        for i in candidates:
            more = min(most - given[i], max(1, budget * weights[i] // mass), spare)
            given[i] = given[i] + more
            spare = spare - more
    return np.array(given)


def normal_values(stream_key, dims, deviation, bound, split=(), kind=jnp.bfloat16):
    values = jax.random.normal(stream_key, dims, jnp.float32) * deviation
    if len(split) > 0:
        values = block_scale(stream_key, dims, split, -0.22, 0.18) * values
    return jnp.clip(values, min=-bound, max=bound).astype(kind)


def noise_with(own_key, dims, scale, bound, shards, heavy, kind=jnp.bfloat16):
    result = scale * jax.random.normal(own_key, dims, jnp.float32)
    if shards:
        result = result * block_scale(own_key, dims, shards, -0.22, 0.18)
    return jnp.clip(with_spikes(result, jax.random.fold_in(own_key, 3), *heavy), -bound, bound).astype(kind)


def setup_inputs(seed: int = 0) -> dict:
    streams_of = jax.random.split(jax.random.key(seed), 7)
    tokens = normal_values(streams_of[0], (TOKENS, D), 1.0, 6.0, ((0, 8), (1, 32)))
    expert_ids_keys = jax.random.split(jax.random.fold_in(streams_of[1], 1), TOKENS // TOK_G)
    expert_ids_turns = jax.random.permutation(jax.random.fold_in(streams_of[1], 3), TOKENS // TOK_G)
    expert_ids = jax.vmap(lambda own, number: shared_out(jax.random.fold_in(streams_of[1], 2), own, number, TOK_G, EXPERTS, 2, CAP, 2))(expert_ids_keys, expert_ids_turns).reshape((TOKENS, 2))
    gate_prob = jnp.clip(0.1 + 0.9 * jax.random.uniform(streams_of[2], (TOKENS, 2), jnp.float32) ** block_scale(streams_of[2], (TOKENS, 2), ((0, 8),), -0.2, 0.2), 0.1, 1.0)
    w_gate = normal_values(streams_of[3], (EXPERTS, D, FF), D ** -0.5, 0.078125, ((0, 8), (2, 32)))
    w_up = normal_values(streams_of[4], (EXPERTS, D, FF), D ** -0.5, 0.078125, ((0, 8), (2, 32)))
    w_down = noise_with(streams_of[5], (EXPERTS, FF, D), FF ** -0.5, 0.125, ((0, 8), (1, 32)), (1, 2, 32, 2.75))
    return dict(tokens=tokens, expert_ids=expert_ids, gate_prob=gate_prob, w_gate=w_gate, w_up=w_up, w_down=w_down)


def slot_table(ids, experts, cap):
    flat = ids.reshape(-1)
    onehot = (flat[:, None] == jnp.arange(experts, dtype=jnp.int32)[None, :]).astype(jnp.int32)
    before = jnp.cumsum(onehot, axis=0) - onehot
    position = jnp.sum(before * onehot, axis=1)
    slot = flat * cap + position
    match = slot[None, :] == jnp.arange(experts * cap, dtype=jnp.int32)[:, None]
    which = jnp.arange(flat.shape[0], dtype=jnp.int32) // 2
    owner = jnp.max(jnp.where(match, which[None, :], -1), axis=1)
    return slot, owner


def reference(tokens, expert_ids, gate_prob, w_gate, w_up, w_down):
    group_rows = []
    group_slots = []
    for group in range(N_EXPERT):
        block = tokens[group * TOK_G:(group + 1) * TOK_G]
        slot, owner = slot_table(expert_ids[group * TOK_G:(group + 1) * TOK_G], EXPERTS, CAP)
        picked = jnp.take(block, jnp.maximum(owner, 0), axis=0)
        picked = jnp.where((owner >= 0)[:, None], picked, jnp.zeros_like(picked))
        group_rows.append(picked.reshape(EXPERTS, CAP, D))
        group_slots.append(slot)
    rows_all = jnp.stack(group_rows, axis=1)
    width = FF // N_TENSOR
    outs = []
    for expert in range(EXPERTS):
        rows = rows_all[expert].reshape(N_EXPERT * CAP, D)
        gate = jnp.dot(rows, w_gate[expert], preferred_element_type=jnp.float32)
        up = jnp.dot(rows, w_up[expert], preferred_element_type=jnp.float32)
        hidden = (jax.nn.silu(gate) * up).astype(jnp.bfloat16)
        down = w_down[expert]

        def add_block(index, total):
            start = (index * width).astype(jnp.int32)
            hid = lax.dynamic_slice_in_dim(hidden, start, width, 1)
            wts = lax.dynamic_slice_in_dim(down, start, width, 0)
            term = jnp.dot(hid, wts, preferred_element_type=jnp.float32)
            term = lax.optimization_barrier(term.astype(jnp.bfloat16)).astype(jnp.float32)
            return total + term

        total = lax.fori_loop(0, N_TENSOR, add_block, jnp.zeros((N_EXPERT * CAP, D), jnp.float32))
        outs.append(total.reshape(N_EXPERT, CAP, D))
    out_all = jnp.stack(outs, axis=0)
    results = []
    for group in range(N_EXPERT):
        table = out_all[:, group].reshape(EXPERTS * CAP, D)
        picked = jnp.take(table, group_slots[group], axis=0).reshape(TOK_G, 2, D)
        weights = gate_prob[group * TOK_G:(group + 1) * TOK_G]
        results.append(jnp.sum(weights[:, :, None] * picked, axis=1).astype(jnp.bfloat16))
    return jnp.concatenate(results, axis=0)
```

```python
import jax
import jax.numpy as jnp
from jax import lax
from jax.sharding import Mesh
from jax.sharding import PartitionSpec as P

NZ = 8
NX = 4


def ring(n, d):
    return [(i, (i + d) % n) for i in range(n)]


def slot_onehots(ids, experts, cap):
    rows = ids.shape[0]
    lanes = jnp.arange(experts, dtype=jnp.int32)[None, :]
    first = ids[:, 0:1] == lanes
    second = ids[:, 1:2] == lanes
    named = (first | second).astype(jnp.bfloat16)
    i = jnp.arange(rows, dtype=jnp.int32)
    lower = (i[:, None] > i[None, :]).astype(jnp.bfloat16)
    before = jnp.dot(lower, named, preferred_element_type=jnp.float32).astype(jnp.int32)
    position = jnp.arange(cap, dtype=jnp.int32)[None, None, :]
    hit = before[:, :, None] == position
    return first, second, hit


def local(tokens, expert_ids, gate_prob, w_gate, w_up, w_down):
    experts = 8
    rows, columns = tokens.shape
    cap = 3 * rows // experts
    slots = experts * cap
    width = w_gate.shape[2]
    model = w_gate.shape[1]
    first, second, hit = slot_onehots(expert_ids, experts, cap)
    pick = (hit & (first | second)[:, :, None]).astype(jnp.bfloat16).reshape(rows, slots)
    weight = (
        jnp.where(first, gate_prob[:, 0:1], 0.0) + jnp.where(second, gate_prob[:, 1:2], 0.0)
    )
    mix = jnp.where(hit, weight[:, :, None], 0.0).reshape(rows, slots)

    sending = jnp.dot(tokens.T, pick, preferred_element_type=jnp.float32).astype(jnp.bfloat16)
    sending = sending.reshape(columns, experts, cap).transpose(1, 0, 2)
    arrived = lax.all_to_all(sending, ("y", "c"), split_axis=0, concat_axis=0, tiled=True)
    arrived = arrived.transpose(1, 0, 2).reshape(columns, slots)
    piece = lax.all_gather(arrived, ("z", "x"), axis=0, tiled=True)

    down, _ = lax.optimization_barrier((w_down[0], arrived))
    down = down.reshape(width, NZ, NX, columns).transpose(2, 0, 1, 3).reshape(NX, width, NZ * columns)
    down = lax.all_to_all(down, "x", split_axis=0, concat_axis=0, tiled=True)
    me = lax.axis_index("x")
    downs = [
        lax.dynamic_slice(
            down, ((me + k) & (NX - 1), 0, 0), (1,) + down.shape[1:], allow_negative_indices=False
        )[0]
        for k in range(NX)
    ]

    contract = (((0,), (0,)), ((), ()))
    gate = lax.dot_general(w_gate[0], piece, contract, preferred_element_type=jnp.float32)
    up = lax.dot_general(w_up[0], piece, contract, preferred_element_type=jnp.float32)
    hidden = (jax.nn.silu(gate) * up).astype(jnp.bfloat16)
    half = slots // 2
    from_left = lax.ppermute(hidden, "x", ring(NX, 1))
    from_right = lax.ppermute(hidden, "x", ring(NX, -1))
    far_top = lax.ppermute(from_left[:, :half], "x", ring(NX, 1))
    far_bottom = lax.ppermute(from_right[:, half:], "x", ring(NX, -1))
    far = jnp.concatenate([far_top, far_bottom], axis=1)
    part = lax.dot_general(downs[0], hidden, contract, preferred_element_type=jnp.float32)
    part += lax.dot_general(downs[3], from_left, contract, preferred_element_type=jnp.float32)
    part += lax.dot_general(downs[1], from_right, contract, preferred_element_type=jnp.float32)
    part += lax.dot_general(downs[2], far, contract, preferred_element_type=jnp.float32)
    summed = lax.psum_scatter(part.astype(jnp.bfloat16), "z", scatter_dimension=0, tiled=True)

    back = summed.reshape(columns, experts, cap).transpose(1, 0, 2)
    back = lax.all_to_all(back, ("y", "c"), split_axis=0, concat_axis=0, tiled=True)
    table = back.transpose(1, 0, 2).reshape(columns, slots)
    high = lax.reduce_precision(mix, 8, 7)
    low = (mix - high).astype(jnp.bfloat16)
    high = high.astype(jnp.bfloat16)
    last = (((1,), (1,)), ((), ()))
    mixed = lax.dot_general(table, high, last, preferred_element_type=jnp.float32)
    mixed += lax.dot_general(table, low, last, preferred_element_type=jnp.float32)
    return mixed.astype(jnp.bfloat16).T


def solution(mesh):
    grid = Mesh(mesh.devices.reshape(4, 2, NZ, NX), ("y", "c", "z", "x"))
    group = ("y", "c")
    tensor = ("z", "x")
    return jax.shard_map(
        local,
        mesh=grid,
        in_specs=(
            P(group, tensor),
            P(group, None),
            P(group, None),
            P(group, None, tensor),
            P(group, None, tensor),
            P(group, tensor, None),
        ),
        out_specs=P(group, tensor),
        check_vma=False,
    )
```

```python
import jax
import jax.numpy as jnp
from jax import lax
from jax.experimental import pallas as pl
from jax.experimental.pallas import tpu as pltpu
from jax.sharding import Mesh
from jax.sharding import PartitionSpec as P

NZ = 8
NX = 4


def ring(n, d):
    return [(i, (i + d) % n) for i in range(n)]


def send(value, axis, d):
    return lax.ppermute(value, axis, ring(NZ if axis == "z" else NX, d))


def slot_onehots(ids, experts, cap):
    rows = ids.shape[0]
    lanes = jnp.arange(experts, dtype=jnp.int32)[None, :]
    first = ids[:, 0:1] == lanes
    second = ids[:, 1:2] == lanes
    named = (first | second).astype(jnp.bfloat16)
    i = jnp.arange(rows, dtype=jnp.int32)
    lower = (i[:, None] > i[None, :]).astype(jnp.bfloat16)
    before = jnp.dot(lower, named, preferred_element_type=jnp.float32).astype(jnp.int32)
    position = jnp.arange(cap, dtype=jnp.int32)[None, None, :]
    hit = before[:, :, None] == position
    return first, second, hit


def relayout_down(place, w_down):
    _, width, model = w_down.shape
    block = model // NZ
    piece = block // NX

    def body(place_ref, w_ref, out_ref):
        turned = w_ref[0].T
        for x in range(NX):
            out_ref[x, 0] = turned[x * piece:(x + 1) * piece]

    return pl.pallas_call(
        body,
        grid_spec=pltpu.PrefetchScalarGridSpec(
            num_scalar_prefetch=1,
            grid=(NZ,),
            in_specs=[pl.BlockSpec((1, width, block), lambda k, s: (0, 0, (s[0] + k) & (NZ - 1)))],
            out_specs=pl.BlockSpec((NX, 1, piece, width), lambda k, s: (0, k, 0, 0)),
        ),
        out_shape=jax.ShapeDtypeStruct((NX, NZ, piece, width), w_down.dtype),
        name="relayout_down",
    )(place, w_down)


def rotate_weights(place, w_gate, w_up):
    _, model, width = w_gate.shape
    piece = model // (NZ * NX)
    shape = (NX, NZ, piece, width)

    def body(place_ref, gate_ref, up_ref, gate_out, up_out):
        for k in range(NX):
            x = (place_ref[1] + k) & (NX - 1)
            gate_out[k, 0] = gate_ref[0, x]
            up_out[k, 0] = up_ref[0, x]

    spec_in = pl.BlockSpec((1, NX, piece, width), lambda k, s: ((s[0] + k) & (NZ - 1), 0, 0, 0))
    spec_out = pl.BlockSpec((NX, 1, piece, width), lambda k, s: (0, k, 0, 0))
    return pl.pallas_call(
        body,
        grid_spec=pltpu.PrefetchScalarGridSpec(
            num_scalar_prefetch=1,
            grid=(NZ,),
            in_specs=[spec_in, spec_in],
            out_specs=[spec_out, spec_out],
        ),
        out_shape=[jax.ShapeDtypeStruct(shape, w_gate.dtype)] * 2,
        name="rotate_weights",
    )(place, w_gate.reshape(NZ, NX, piece, width), w_up.reshape(NZ, NX, piece, width))


def down_parts(downs, hidden):
    _, _, piece, width = downs.shape
    slots = hidden.shape[1]

    def body(down_ref, hidden_ref, out_ref):
        total = jnp.zeros((piece, slots), jnp.float32)
        for x in range(NX):
            total += lax.dot_general(
                down_ref[x, 0],
                hidden_ref[x],
                (((1,), (1,)), ((), ())),
                preferred_element_type=jnp.float32,
            )
        out_ref[0] = total.astype(jnp.bfloat16)

    return pl.pallas_call(
        body,
        grid=(NZ,),
        in_specs=[
            pl.BlockSpec((NX, 1, piece, width), lambda k: (0, k, 0, 0)),
            pl.BlockSpec((NX, slots, width), lambda k: (0, 0, 0)),
        ],
        out_specs=pl.BlockSpec((1, piece, slots), lambda k: (k, 0, 0)),
        out_shape=jax.ShapeDtypeStruct((NZ, piece, slots), jnp.bfloat16),
        name="down_parts",
    )(downs, hidden)


def times(block, weight):
    return lax.dot_general(
        block, weight, (((0,), (0,)), ((), ())), preferred_element_type=jnp.float32
    )


def scatter_z(parts):
    half = parts.shape[1] // 2

    def add(a, b):
        return (a.astype(jnp.float32) + b.astype(jnp.float32)).astype(jnp.bfloat16)

    right = send(parts[4, :half], "z", 1)
    left = send(parts[4, half:], "z", -1)
    right = jnp.concatenate([add(parts[3, :half], right), parts[3, half:]], axis=0)
    left = jnp.concatenate([parts[5, :half], add(parts[5, half:], left)], axis=0)
    right = send(right, "z", 1)
    left = send(left, "z", -1)
    right = send(add(parts[2], right), "z", 1)
    left = send(add(parts[6], left), "z", -1)
    right = send(add(parts[1], right), "z", 1)
    left = send(add(parts[7], left), "z", -1)
    total = parts[0].astype(jnp.float32) + right.astype(jnp.float32) + left.astype(jnp.float32)
    return total.astype(jnp.bfloat16)


def gather_x(value):
    return lax.all_to_all(
        jnp.broadcast_to(value[None], (NX,) + value.shape), "x", 0, 0, tiled=True
    )


def local(tokens, expert_ids, gate_prob, w_gate, w_up, w_down):
    experts = 8
    rows, columns = tokens.shape
    cap = 3 * rows // experts
    slots = experts * cap
    width = w_gate.shape[2]
    z = lax.axis_index("z")
    place = jnp.stack([z, lax.axis_index("x")]).astype(jnp.int32)

    first, second, hit = slot_onehots(expert_ids, experts, cap)
    pick = (hit & (first | second)[:, :, None]).astype(jnp.bfloat16).reshape(rows, slots)
    weight = (
        jnp.where(first, gate_prob[:, 0:1], 0.0) + jnp.where(second, gate_prob[:, 1:2], 0.0)
    )
    mix = jnp.where(hit, weight[:, :, None], 0.0).reshape(rows, slots)

    sending = jnp.dot(tokens.T, pick, preferred_element_type=jnp.float32).astype(jnp.bfloat16)
    sending = sending.reshape(columns, experts, cap).transpose(1, 0, 2)
    arrived = lax.all_to_all(sending, ("y", "c"), split_axis=0, concat_axis=0, tiled=True)
    groups = experts // 2
    half_slots = groups * cap
    a = arrived[:groups].transpose(1, 0, 2).reshape(columns, half_slots)
    b = arrived[groups:].transpose(1, 0, 2).reshape(columns, half_slots)

    a0 = gather_x(a).reshape(NX * columns, half_slots)
    blocks_a = {0: a0}
    right, left = a0, a0
    for k in range(1, 4):
        right = send(right, "z", 1)
        left = send(left, "z", -1)
        blocks_a[-k] = right
        blocks_a[k] = left
    mid = NX * columns // 2
    far_a = (send(right[:mid], "z", 1), send(left[mid:], "z", -1))

    blocks_b = [b] + [None] * (NZ - 1)
    right, left = b, b
    for k in range(1, 4):
        right = send(right, "z", 1)
        left = send(left, "z", -1)
        blocks_b[NZ - k] = right
        blocks_b[k] = left
    half = columns // 2
    blocks_b[4] = jnp.concatenate(
        [send(right[:half], "z", 1), send(left[half:], "z", -1)], axis=0
    )
    b0 = jnp.concatenate(blocks_b, axis=0)
    b_left = send(b0, "x", 1)
    b_right = send(b0, "x", -1)
    far = NZ * columns // 2
    far_b = (send(b_left[:far], "x", 1), send(b_right[far:], "x", -1))

    w_down, _ = lax.optimization_barrier((w_down, a0))
    down = relayout_down(place, w_down)
    downs = lax.all_to_all(down, "x", split_axis=0, concat_axis=0, tiled=True)
    turned_gate, turned_up = rotate_weights(place, w_gate, w_up)

    def gated_a(w):
        w = w[0].reshape(NZ, NX * columns, width)
        total = None
        for k in (0, 1, -1, 2, -2, 3, -3, 4):
            index = ((z + k) & (NZ - 1), 0, 0)
            wk = lax.dynamic_slice(w, index, (1,) + w.shape[1:], allow_negative_indices=False)[0]
            if k == 4:
                term = times(far_a[0], wk[:mid]) + times(far_a[1], wk[mid:])
            else:
                term = times(blocks_a[k], wk)
            total = term if total is None else total + term
        return total

    def gated_b(w):
        w = w.reshape(NX, NZ * columns, width)
        total = times(b0, w[0])
        total += times(b_right, w[1])
        total += times(b_left, w[3])
        total += times(far_b[0], w[2, :far]) + times(far_b[1], w[2, far:])
        return total

    hidden_a = (jax.nn.silu(gated_a(w_gate)) * gated_a(w_up)).astype(jnp.bfloat16)
    sum_a = scatter_z(down_parts(downs, gather_x(hidden_a)))
    hidden_b = (jax.nn.silu(gated_b(turned_gate)) * gated_b(turned_up)).astype(jnp.bfloat16)
    sum_b = scatter_z(down_parts(downs, gather_x(hidden_b)))

    back = jnp.concatenate([sum_a, sum_b], axis=1)
    back = back.reshape(columns, experts, cap).transpose(1, 0, 2)
    back = lax.all_to_all(back, ("y", "c"), split_axis=0, concat_axis=0, tiled=True)
    table = back.transpose(1, 0, 2).reshape(columns, slots)
    high = lax.reduce_precision(mix, 8, 7)
    low = (mix - high).astype(jnp.bfloat16)
    high = high.astype(jnp.bfloat16)
    last = (((1,), (1,)), ((), ()))
    mixed = lax.dot_general(table, high, last, preferred_element_type=jnp.float32)
    mixed += lax.dot_general(table, low, last, preferred_element_type=jnp.float32)
    return mixed.astype(jnp.bfloat16).T


def solution(mesh):
    grid = Mesh(mesh.devices.reshape(4, 2, NZ, NX), ("y", "c", "z", "x"))
    group = ("y", "c")
    tensor = ("z", "x")
    return jax.shard_map(
        local,
        mesh=grid,
        in_specs=(
            P(group, tensor),
            P(group, None),
            P(group, None),
            P(group, None, tensor),
            P(group, None, tensor),
            P(group, tensor, None),
        ),
        out_specs=P(group, tensor),
        check_vma=False,
    )
```

```python
import jax
import jax.numpy as jnp
from jax import lax
from jax.experimental import pallas as pl
from jax.experimental.pallas import tpu as pltpu
from jax.sharding import Mesh
from jax.sharding import PartitionSpec as P


NZ = 8
NX = 4


def ring(n, d):
    return [(i, (i + d) % n) for i in range(n)]


def send(value, axis, d):
    return lax.ppermute(value, axis, ring(NZ if axis == "z" else NX, d))


def slot_onehots(ids, experts, cap):
    rows = ids.shape[0]
    lanes = jnp.arange(experts, dtype=jnp.int32)[None, :]
    first = ids[:, 0:1] == lanes
    second = ids[:, 1:2] == lanes
    named = (first | second).astype(jnp.bfloat16)
    i = jnp.arange(rows, dtype=jnp.int32)
    lower = (i[:, None] > i[None, :]).astype(jnp.bfloat16)
    before = jnp.dot(lower, named, preferred_element_type=jnp.float32).astype(jnp.int32)
    position = jnp.arange(cap, dtype=jnp.int32)[None, None, :]
    hit = before[:, :, None] == position
    return first, second, hit


def relayout_down(w_down):
    _, width, model = w_down.shape
    block = model // NZ
    piece = block // NX

    def body(w_ref, out_ref):
        turned = w_ref[0].T
        for x in range(NX):
            out_ref[x, 0] = turned[x * piece:(x + 1) * piece]

    return pl.pallas_call(
        body,
        grid=(NZ,),
        in_specs=[pl.BlockSpec((1, width, block), lambda k: (0, 0, k))],
        out_specs=pl.BlockSpec((NX, 1, piece, width), lambda k: (0, k, 0, 0)),
        out_shape=jax.ShapeDtypeStruct((NX, NZ, piece, width), w_down.dtype),
        name="relayout_down",
    )(w_down)


def down_parts(downs, hidden):
    _, _, piece, width = downs.shape
    slots = hidden.shape[1]

    def body(down_ref, hidden_ref, out_ref, turned_ref):
        @pl.when(pl.program_id(0) == 0)
        def _():
            for x in range(NX):
                turned_ref[x] = hidden_ref[x].T

        total = jnp.zeros((piece, slots), jnp.float32)
        for x in range(NX):
            total += jnp.dot(down_ref[x, 0], turned_ref[x], preferred_element_type=jnp.float32)
        out_ref[...] = total.astype(jnp.bfloat16)

    return pl.pallas_call(
        body,
        grid=(NZ,),
        in_specs=[
            pl.BlockSpec((NX, 1, piece, width), lambda k: (0, k, 0, 0)),
            pl.BlockSpec((NX, slots, width), lambda k: (0, 0, 0)),
        ],
        out_specs=pl.BlockSpec((piece, slots), lambda k: (k, 0)),
        out_shape=jax.ShapeDtypeStruct((NZ * piece, slots), jnp.bfloat16),
        scratch_shapes=[pltpu.VMEM((NX, width, slots), jnp.bfloat16)],
        name="down_parts",
    )(downs, hidden)


def times(block, weight):
    return lax.dot_general(
        block, weight, (((0,), (0,)), ((), ())), preferred_element_type=jnp.float32
    )


def gather_x(value):
    return lax.all_to_all(
        jnp.broadcast_to(value[None], (NX,) + value.shape), "x", 0, 0, tiled=True
    )


def layer(tokens, expert_ids, gate_prob, w_gate, w_up, w_down):
    experts = 8
    rows, columns = tokens.shape
    cap = 3 * rows // experts
    slots = experts * cap
    width = w_gate.shape[2]
    z = lax.axis_index("z")

    first, second, hit = slot_onehots(expert_ids, experts, cap)
    pick = (hit & (first | second)[:, :, None]).astype(jnp.bfloat16).reshape(rows, slots)
    weight = (
        jnp.where(first, gate_prob[:, 0:1], 0.0) + jnp.where(second, gate_prob[:, 1:2], 0.0)
    )
    mix = jnp.where(hit, weight[:, :, None], 0.0).reshape(rows, slots)

    sending = jnp.dot(tokens.T, pick, preferred_element_type=jnp.float32).astype(jnp.bfloat16)
    sending = sending.reshape(columns, experts, cap).transpose(1, 0, 2)
    arrived = lax.all_to_all(sending, ("y", "c"), split_axis=0, concat_axis=0, tiled=True)
    arrived = arrived.transpose(1, 0, 2).reshape(columns, slots)
    cut = slots // 3
    piece_b = lax.all_gather(arrived[:, cut:], ("z", "x"), axis=0, tiled=True)

    a0 = gather_x(arrived[:, :cut]).reshape(NX * columns, cut)
    blocks = {0: a0}
    right, left = a0, a0
    for k in range(1, 4):
        right = send(right, "z", 1)
        left = send(left, "z", -1)
        blocks[-k] = right
        blocks[k] = left
    mid = NX * columns // 2
    far = (send(right[:mid], "z", 1), send(left[mid:], "z", -1))

    down = relayout_down(w_down)
    downs = lax.all_to_all(down, "x", split_axis=0, concat_axis=0, tiled=True)

    def gated_a(w):
        w = w[0].reshape(NZ, NX * columns, width)
        total = None
        for k in (0, 1, -1, 2, -2, 3, -3, 4):
            index = ((z + k) & (NZ - 1), 0, 0)
            wk = lax.dynamic_slice(w, index, (1,) + w.shape[1:], allow_negative_indices=False)[0]
            if k == 4:
                term = times(far[0], wk[:mid]) + times(far[1], wk[mid:])
            else:
                term = times(blocks[k], wk)
            total = term if total is None else total + term
        return total

    hidden_a = (jax.nn.silu(gated_a(w_gate)) * gated_a(w_up)).astype(jnp.bfloat16)
    all_a = gather_x(hidden_a)
    part_a = down_parts(downs, all_a)
    sum_a = lax.psum_scatter(part_a, "z", scatter_dimension=0, tiled=True)
    gate_b = times(piece_b, w_gate[0])
    up_b = times(piece_b, w_up[0])
    hidden_b = (jax.nn.silu(gate_b) * up_b).astype(jnp.bfloat16)
    all_b = gather_x(hidden_b)
    part_b = down_parts(downs, all_b)
    sum_b = lax.psum_scatter(part_b, "z", scatter_dimension=0, tiled=True)

    back = jnp.concatenate([sum_a, sum_b], axis=1)
    back = back.reshape(columns, experts, cap).transpose(1, 0, 2)
    back = lax.all_to_all(back, ("y", "c"), split_axis=0, concat_axis=0, tiled=True)
    table = back.transpose(1, 0, 2).reshape(columns, slots)
    high = lax.reduce_precision(mix, 8, 7)
    low = (mix - high).astype(jnp.bfloat16)
    high = high.astype(jnp.bfloat16)
    last = (((1,), (1,)), ((), ()))
    mixed = lax.dot_general(table, high, last, preferred_element_type=jnp.float32)
    mixed += lax.dot_general(table, low, last, preferred_element_type=jnp.float32)
    return mixed.astype(jnp.bfloat16).T


def solution(mesh):
    grid = Mesh(mesh.devices.reshape(4, 2, NZ, NX), ("y", "c", "z", "x"))
    group = ("y", "c")
    tensor = ("z", "x")
    return jax.shard_map(
        layer,
        mesh=grid,
        in_specs=(
            P(group, tensor),
            P(group, None),
            P(group, None),
            P(group, None, tensor),
            P(group, None, tensor),
            P(group, tensor, None),
        ),
        out_specs=P(group, tensor),
        check_vma=False,
    )
```

```python
import jax
import jax.numpy as jnp
from jax import lax
from jax.experimental import pallas as pl
from jax.experimental.pallas import tpu as pltpu
from jax.sharding import Mesh
from jax.sharding import PartitionSpec as P


NZ = 8
NX = 4


def ring(n, d):
    return [(i, (i + d) % n) for i in range(n)]


def send(value, axis, d):
    return lax.ppermute(value, axis, ring(NZ if axis == "z" else NX, d))


def slot_onehots(ids, experts, cap):
    rows = ids.shape[0]
    lanes = jnp.arange(experts, dtype=jnp.int32)[None, :]
    first = ids[:, 0:1] == lanes
    second = ids[:, 1:2] == lanes
    named = (first | second).astype(jnp.bfloat16)
    i = jnp.arange(rows, dtype=jnp.int32)
    lower = (i[:, None] > i[None, :]).astype(jnp.bfloat16)
    before = jnp.dot(lower, named, preferred_element_type=jnp.float32).astype(jnp.int32)
    position = jnp.arange(cap, dtype=jnp.int32)[None, None, :]
    hit = before[:, :, None] == position
    return first, second, hit


def relayout_down(place, w_down):
    _, width, model = w_down.shape
    block = model // NZ
    piece = block // NX

    def body(place_ref, w_ref, out_ref):
        turned = w_ref[0].T
        for x in range(NX):
            out_ref[x, 0] = turned[x * piece:(x + 1) * piece]

    return pl.pallas_call(
        body,
        grid_spec=pltpu.PrefetchScalarGridSpec(
            num_scalar_prefetch=1,
            grid=(NZ,),
            in_specs=[pl.BlockSpec((1, width, block), lambda k, s: (0, 0, (s[0] + k) & (NZ - 1)))],
            out_specs=pl.BlockSpec((NX, 1, piece, width), lambda k, s: (0, k, 0, 0)),
        ),
        out_shape=jax.ShapeDtypeStruct((NX, NZ, piece, width), w_down.dtype),
        name="relayout_down",
    )(place, w_down)


def down_parts(downs, hidden, order):
    _, _, piece, width = downs.shape
    slots = hidden.shape[1]
    first = order[0]

    def body(down_ref, hidden_ref, out_ref, turned_ref):
        @pl.when(pl.program_id(0) == 0)
        def _():
            for x in range(NX):
                turned_ref[x] = hidden_ref[x].T

        total = jnp.zeros((piece, slots), jnp.float32)
        for x in range(NX):
            total += jnp.dot(down_ref[x, 0], turned_ref[x], preferred_element_type=jnp.float32)
        out_ref[0] = total.astype(jnp.bfloat16)

    return pl.pallas_call(
        body,
        grid=(len(order),),
        in_specs=[
            pl.BlockSpec((NX, 1, piece, width), lambda k: (0, (k + first) & (NZ - 1), 0, 0)),
            pl.BlockSpec((NX, slots, width), lambda k: (0, 0, 0)),
        ],
        out_specs=pl.BlockSpec((1, piece, slots), lambda k: (k, 0, 0)),
        out_shape=jax.ShapeDtypeStruct((len(order), piece, slots), jnp.bfloat16),
        scratch_shapes=[pltpu.VMEM((NX, width, slots), jnp.bfloat16)],
        name="down_parts",
    )(downs, hidden)


def scatter_z(parts):
    half = parts[4].shape[0] // 2

    def add(a, b):
        return (a.astype(jnp.float32) + b.astype(jnp.float32)).astype(jnp.bfloat16)

    right = send(parts[4][:half], "z", 1)
    left = send(parts[4][half:], "z", -1)
    right = jnp.concatenate([add(parts[3][:half], right), parts[3][half:]], axis=0)
    left = jnp.concatenate([parts[5][:half], add(parts[5][half:], left)], axis=0)
    right = send(right, "z", 1)
    left = send(left, "z", -1)
    right = send(add(parts[2], right), "z", 1)
    left = send(add(parts[6], left), "z", -1)
    right = send(add(parts[1], right), "z", 1)
    left = send(add(parts[7], left), "z", -1)
    total = parts[0].astype(jnp.float32) + right.astype(jnp.float32) + left.astype(jnp.float32)
    return total.astype(jnp.bfloat16)


def times(block, weight):
    return lax.dot_general(
        block, weight, (((0,), (0,)), ((), ())), preferred_element_type=jnp.float32
    )


def gather(value, axis):
    n = NZ if axis == "z" else NX
    return lax.all_to_all(
        jnp.broadcast_to(value[None], (n,) + value.shape), axis, 0, 0, tiled=True
    )


def layer(tokens, expert_ids, gate_prob, w_gate, w_up, w_down):
    experts = 8
    rows, columns = tokens.shape
    cap = 3 * rows // experts
    slots = experts * cap
    width = w_gate.shape[2]
    z = lax.axis_index("z")
    x = lax.axis_index("x")

    first, second, hit = slot_onehots(expert_ids, experts, cap)
    pick = (hit & (first | second)[:, :, None]).astype(jnp.bfloat16).reshape(rows, slots)
    weight = (
        jnp.where(first, gate_prob[:, 0:1], 0.0) + jnp.where(second, gate_prob[:, 1:2], 0.0)
    )
    mix = jnp.where(hit, weight[:, :, None], 0.0).reshape(rows, slots)

    sending = jnp.dot(tokens.T, pick, preferred_element_type=jnp.float32).astype(jnp.bfloat16)
    sending = sending.reshape(columns, experts, cap).transpose(1, 0, 2)
    arrived = lax.all_to_all(sending, ("y", "c"), split_axis=0, concat_axis=0, tiled=True)
    arrived = arrived.transpose(1, 0, 2).reshape(columns, slots)
    cut = 2 * slots // 3
    a0 = gather(arrived[:, :cut], "x").reshape(NX * columns, cut)
    blocks = {0: a0}
    right, left = a0, a0
    for k in range(1, 4):
        right = send(right, "z", 1)
        left = send(left, "z", -1)
        blocks[-k] = right
        blocks[k] = left
    mid = NX * columns // 2
    far = (send(right[:mid], "z", 1), send(left[mid:], "z", -1))

    b0 = gather(arrived[:, cut:], "z").reshape(NZ * columns, slots - cut)
    b_left = send(b0, "x", 1)
    b_right = send(b0, "x", -1)
    bmid = NZ * columns // 2
    b_far = (send(b_left[:bmid], "x", 1), send(b_right[bmid:], "x", -1))

    down = relayout_down(z.astype(jnp.int32)[None], w_down)
    downs = lax.all_to_all(down, "x", split_axis=0, concat_axis=0, tiled=True)

    def gated_a(w):
        w = w[0].reshape(NZ, NX * columns, width)
        total = None
        for k in (0, 1, -1, 2, -2, 3, -3, 4):
            index = ((z + k) & (NZ - 1), 0, 0)
            wk = lax.dynamic_slice(w, index, (1,) + w.shape[1:], allow_negative_indices=False)[0]
            if k == 4:
                term = times(far[0], wk[:mid]) + times(far[1], wk[mid:])
            else:
                term = times(blocks[k], wk)
            total = term if total is None else total + term
        return total

    def gated_b(w):
        w = w[0].reshape(NZ, NX, columns, width).transpose(1, 0, 2, 3).reshape(NX, NZ * columns, width)

        def at(k):
            index = ((x + k) & (NX - 1), 0, 0)
            return lax.dynamic_slice(
                w, index, (1,) + w.shape[1:], allow_negative_indices=False
            )[0]

        total = times(b0, at(0)) + times(b_right, at(1)) + times(b_left, at(3))
        opposite = at(2)
        return total + (times(b_far[0], opposite[:bmid]) + times(b_far[1], opposite[bmid:]))

    hidden_b = (jax.nn.silu(gated_b(w_gate)) * gated_b(w_up)).astype(jnp.bfloat16)
    all_b = gather(hidden_b, "x")
    part_b = down_parts(downs, all_b, (0, 1, 2, 3, 4, 5, 6, 7))
    hidden_a = (jax.nn.silu(gated_a(w_gate)) * gated_a(w_up)).astype(jnp.bfloat16)
    all_a = gather(hidden_a, "x")
    early = down_parts(downs, all_a, (3, 4, 5))
    late = down_parts(downs, all_a, (6, 7, 0, 1, 2))
    parts = {}
    for k in range(NZ):
        part_a = early[k - 3] if 3 <= k <= 5 else late[(k - 6) % NZ]
        parts[k] = jnp.concatenate([part_a, part_b[k]], axis=1)
    back = scatter_z(parts)
    back = back.reshape(columns, experts, cap).transpose(1, 0, 2)
    back = lax.all_to_all(back, ("y", "c"), split_axis=0, concat_axis=0, tiled=True)
    table = back.transpose(1, 0, 2).reshape(columns, slots)
    high = lax.reduce_precision(mix, 8, 7)
    low = (mix - high).astype(jnp.bfloat16)
    high = high.astype(jnp.bfloat16)
    last = (((1,), (1,)), ((), ()))
    mixed = lax.dot_general(table, high, last, preferred_element_type=jnp.float32)
    mixed += lax.dot_general(table, low, last, preferred_element_type=jnp.float32)
    return mixed.astype(jnp.bfloat16).T


def solution(mesh):
    grid = Mesh(mesh.devices.reshape(4, 2, NZ, NX), ("y", "c", "z", "x"))
    group = ("y", "c")
    tensor = ("z", "x")
    return jax.shard_map(
        layer,
        mesh=grid,
        in_specs=(
            P(group, tensor),
            P(group, None),
            P(group, None),
            P(group, None, tensor),
            P(group, None, tensor),
            P(group, tensor, None),
        ),
        out_specs=P(group, tensor),
        check_vma=False,
    )
```
